256 devices in a mesh: gx: 16 (over z, core), gy: 16 (over y, x).
Axes of the slice: x: 4, y: 4, z: 8, core: 2. Of those that a mesh axis runs over, the one named last changes fastest.
Arguments:
- fine_state: float32 [9, 8, 256, 4096], P(None, None, 'gx', 'gy'), may hold values from -6 to 6
- coarse_column_state: float32 [3, 9, 12, 128, 2048], P(None, None, None, 'gx', 'gy'), may hold values from -6 to 6
- diffusivity: float32 [9], replicated, may hold values from 0.02 to 0.08
- rates: float32 [9, 9], replicated, may hold values from -0.4 to 0.4
- owner_offset: int32 [16, 16], replicated, may hold values from -1 to 1
Outputs:
- fine_new: float32 [9, 8, 256, 4096], P(None, None, 'gx', 'gy')
- coarse_new: float32 [3, 9, 12, 128, 2048], P(None, None, None, 'gx', 'gy')
The draws below stay inside these ranges and needn't reach their ends.
Inputs may be any that keep to these rules, and one draw needn't show every extreme that they name: The coarse column over fine box (i, j) lies in slot 1 - owner_offset[i, j] of the block at gy index (j + owner_offset[i, j]) mod 16 in the same gx row; a block owns zero to three columns.
All inputs are finite; a program needn't handle non-finite values.
Results may differ from the reference program's by a relative error of at most 0.0001.
Values sent between devices are 32-bit elements; how exact they have to be, the bound alone decides.
No kernel may reach another device: no remote copies, remote signals or barrier semaphores. Data moves between devices by JAX's collectives and lax.ppermute only.
A program may use at most 128 MiB of HBM per device.

```python
import math
import jax
import jax.numpy as jnp
from jax import lax

NF = 9
FZ = 8
CZ = 12
NBX = 16
NBY = 16
FXG = 256
FYG = 4096
CXG = 128
CYG = 2048


def set_ends(values, rng, low, largest):
    dims = values.shape
    place = [jax.random.randint(jax.random.fold_in(rng, axis), (), 0, dims[axis]) for axis in range(len(dims))]
    values = values.at[tuple(place)].set(low)
    longest = dims.index(max(dims))
    place[longest] = (place[longest] + 1) % dims[longest]
    return values.at[tuple(place)].set(largest)


def steps_of(key, dims, shards, low, high):
    def one(axis_at, parts):
        heights = jax.random.uniform(jax.random.fold_in(jax.random.fold_in(key, 6), axis_at), (parts,), jnp.float32, low / len(shards), high / len(shards))
        return jnp.repeat(jnp.exp(heights), dims[axis_at] // parts).reshape((-1,) + (1,) * (len(dims) - axis_at - 1))

    factor_of = one(*shards[0])
    for cut in shards[1:]:
        factor_of = factor_of * one(*cut)
    return factor_of


def centred(rng, shape, width, bound, shards=(), kind=jnp.bfloat16):
    array = width * jax.random.normal(rng, shape, jnp.float32)
    if shards:
        array = array * steps_of(rng, shape, shards, -0.22, 0.18)
    return jnp.clip(array, -bound, bound).astype(kind)


def setup_inputs(seed: int = 0) -> dict:
    keys = jax.random.split(jax.random.key(seed), 6)
    return {
        "fine_state": centred(keys[0], (NF, FZ, FXG, FYG), 1.0, 6.0, ((2, 16), (3, 16)), jnp.float32),
        "coarse_column_state": centred(keys[1], (3, NF, CZ, CXG, CYG), 1.0, 6.0, ((3, 16), (4, 16)), jnp.float32),
        "diffusivity": jnp.clip(jnp.exp(jax.random.uniform(keys[2], (NF,), jnp.float32, math.log(0.02), math.log(0.08))), 0.02, 0.08),
        "rates": centred(keys[3], (NF, NF), 0.1, 0.4, (), jnp.float32),
        "owner_offset": set_ends(jax.random.randint(keys[4], (NBX, NBY), -1, 2), jax.random.fold_in(keys[4], 1), -1, 1).astype(jnp.int32),
    }


coarse_dt = 1.0
fine_dt = 0.5
fine_inv_h = 2.0
fine_inv_h2 = 4.0


def react(field, rates):
    return jnp.einsum("fg,...gzxy->...fzxy", rates, field, precision=lax.Precision.HIGHEST)


def coarse_step(column, diffusivity, rates):
    faces = -diffusivity[:, None, None, None] * (column[..., 1:, :, :] - column[..., :-1, :, :])
    zero = jnp.zeros_like(faces[..., :1, :, :])
    padded = jnp.concatenate([zero, faces, zero], axis=-3)
    change = -(padded[..., 1:, :, :] - padded[..., :-1, :, :]) + react(column, rates)
    return column + coarse_dt * change, faces


def refine(ghost):
    return jnp.repeat(jnp.repeat(ghost, 2, axis=-2), 2, axis=-1)


def coarsen(flux):
    field_count, nx, ny = flux.shape
    return jnp.sum(flux.reshape(field_count, nx // 2, 2, ny // 2, 2), axis=(2, 4)) * 0.25


def average(field):
    field_count, vertical_count, nx, ny = field.shape
    return jnp.sum(field.reshape(field_count, vertical_count // 2, 2, nx // 2, 2, ny // 2, 2), axis=(2, 4, 6)) * 0.125


def finish(advanced, faces, averaged, low_sum, high_sum):
    vertical_count = advanced.shape[1]
    nslab = averaged.shape[1]
    lower = (vertical_count - nslab) // 2
    upper = lower + nslab
    fix_low = advanced[:, lower - 1] + coarse_dt * faces[:, lower - 1] - low_sum
    fix_high = advanced[:, upper] - coarse_dt * faces[:, upper - 1] + high_sum
    return jnp.concatenate([advanced[:, :lower - 1], fix_low[:, None], averaged, fix_high[:, None], advanced[:, upper + 1:]], axis=1)


def fine_step(field, side_sum, low, high, diffusivity, rates):
    vert = jnp.concatenate([low[:, None], field, high[:, None]], axis=1)
    near = vert[:, 2:] + vert[:, :-2] + side_sum
    kappa = diffusivity[:, None, None, None]
    new = field + fine_dt * (fine_inv_h2 * kappa * (near - 6.0 * field) + react(field, rates))
    flux_low = -fine_inv_h * diffusivity[:, None, None] * (field[:, 0] - low)
    flux_high = -fine_inv_h * diffusivity[:, None, None] * (high - field[:, -1])
    return new, flux_low, flux_high


def sides(field):
    return (jnp.roll(field, -1, 2) + jnp.roll(field, 1, 2)) + (jnp.roll(field, -1, 3) + jnp.roll(field, 1, 3))


def reference(fine_state, coarse_column_state, diffusivity, rates, owner_offset):
    slot_count, field_count, vertical_count, coarse_x_ghosted, coarse_y_ghosted = coarse_column_state.shape
    block_count_x, block_count_y = owner_offset.shape
    coarse_x_block = coarse_x_ghosted // block_count_x
    coarse_y_block = coarse_y_ghosted // block_count_y
    block_grid = coarse_column_state.reshape(slot_count, field_count, vertical_count, block_count_x, coarse_x_block, block_count_y, coarse_y_block)
    rows_idx = jnp.arange(block_count_x, dtype=jnp.int32)[:, None]
    owners = (jnp.arange(block_count_y, dtype=jnp.int32)[None, :] + owner_offset.astype(jnp.int32)) % block_count_y
    slots = (1 - owner_offset).astype(jnp.int32)
    picked = block_grid[slots, :, :, rows_idx, :, owners, :]
    columns = picked.transpose(2, 3, 0, 4, 1, 5).reshape(field_count, vertical_count, coarse_x_ghosted, coarse_y_ghosted)
    advanced, faces = coarse_step(columns, diffusivity, rates)
    nslab = fine_state.shape[1] // 2
    lower = (vertical_count - nslab) // 2
    upper = lower + nslab
    ghost_old = (columns[:, lower - 1], columns[:, upper])
    ghost_mid = (0.5 * (columns[:, lower - 1] + advanced[:, lower - 1]), 0.5 * (columns[:, upper] + advanced[:, upper]))
    field = fine_state
    total_low = jnp.zeros(fine_state.shape[0:1] + fine_state.shape[2:], jnp.float32)
    total_high = jnp.zeros(fine_state.shape[0:1] + fine_state.shape[2:], jnp.float32)
    for ghosts in (ghost_old, ghost_mid):
        field, flux_low, flux_high = fine_step(field, sides(field), refine(ghosts[0]), refine(ghosts[1]), diffusivity, rates)
        total_low = total_low + fine_dt * flux_low
        total_high = total_high + fine_dt * flux_high
    final = finish(advanced, faces, average(field), coarsen(total_low), coarsen(total_high))
    back = final.reshape(field_count, vertical_count, block_count_x, coarse_x_block, block_count_y, coarse_y_block).transpose(2, 4, 0, 1, 3, 5)
    coarse_new = block_grid.at[slots, :, :, rows_idx, :, owners, :].set(back).reshape(coarse_column_state.shape)
    return field, coarse_new
```

```python
import jax
import jax.numpy as jnp
from jax import lax
from jax.experimental import pallas as pl
from jax.experimental.pallas import tpu as pltpu
from jax.sharding import PartitionSpec as P

F32 = jnp.float32
BF16 = jnp.bfloat16
NF = 9
NZ = 8
NX = 16
NY = 256
LOW = 3
HIGH = 8
VMEM = pltpu.VMEM
SMEM = pltpu.SMEM


def call(kernel, name, outs, spaces, flops, limit=8, aliases=None, scratch=(), out_spaces=None):
    return pl.pallas_call(
        kernel,
        name=name,
        out_shape=[jax.ShapeDtypeStruct(s, F32) for s in outs],
        in_specs=[pl.BlockSpec(memory_space=s) for s in spaces],
        out_specs=[pl.BlockSpec(memory_space=s) for s in out_spaces or [VMEM] * len(outs)],
        scratch_shapes=list(scratch),
        input_output_aliases=aliases or {},
        compiler_params=pltpu.CompilerParams(vmem_limit_bytes=limit << 20),
        cost_estimate=pl.CostEstimate(flops=flops, bytes_accessed=1 << 20, transcendentals=0),
    )


def spread_table():
    coarse = lax.broadcasted_iota(jnp.int32, (128, 256), 0)
    fine = lax.broadcasted_iota(jnp.int32, (128, 256), 1)
    return jnp.where(lax.shift_right_logical(fine, 1) == coarse, 1.0, 0.0).astype(BF16)


def gather_table():
    fine = lax.broadcasted_iota(jnp.int32, (256, 128), 0)
    coarse = lax.broadcasted_iota(jnp.int32, (256, 128), 1)
    return jnp.where(lax.shift_right_logical(fine, 1) == coarse, 1.0, 0.0).astype(BF16)


def table_dot(value, table):
    high = value.astype(BF16)
    low = (value - high.astype(F32)).astype(BF16)
    return jnp.dot(high, table, preferred_element_type=F32) + jnp.dot(
        low, table, preferred_element_type=F32
    )


def reacted(tiles, f, scale, diagonal, rates):
    total = tiles[f] * (diagonal + scale * rates[f, f])
    for g in range(NF):
        if g != f:
            total = total + tiles[g] * (scale * rates[f, g])
    return total


def pack_columns(ref, side):
    lane = lax.broadcasted_iota(jnp.int32, (NX, 128), 1)
    packed = jnp.zeros((NX, 128), F32)
    for z in range(NZ):
        for f in range(NF):
            at = z * 16 + f
            tile = ref[f, side, z * NX : (z + 1) * NX, :]
            shift = at if side == 0 else (at - 127) % 128
            moved = pltpu.roll(tile, shift, 1) if shift else tile
            packed = jnp.where(lane == at, moved, packed)
    return packed


def kappa_lanes(kap):
    lane = lax.broadcasted_iota(jnp.int32, (NX, 128), 1) & 15
    out = jnp.zeros((NX, 128), F32)
    for f in range(NF):
        out = jnp.where(lane == f, 2.0 * kap[f], out)
    return out


def add_columns(ref, left, right):
    lane = lax.broadcasted_iota(jnp.int32, (NX, 128), 1)
    for z in range(NZ):
        rows = slice(z * NX, (z + 1) * NX)
        for f in range(NF):
            at = z * 16 + f
            moved = pltpu.roll(left, 128 - at, 1) if at else left
            ref[f, 0, rows, :] = ref[f, 0, rows, :] + jnp.where(lane == 0, moved, 0.0)
            shift = 127 - at
            moved = pltpu.roll(right, shift, 1) if shift else right
            ref[f, 1, rows, :] = ref[f, 1, rows, :] + jnp.where(lane == 127, moved, 0.0)


def row_of(ref, f, half, row):
    return ref[f, half, pl.ds(row, NZ, stride=NX), :]


def set_row(ref, f, half, row, value):
    ref[f, half, pl.ds(row, NZ, stride=NX), :] = value


def plane_at(z):
    start = z * NX
    return pl.ds(start if isinstance(z, int) else pl.multiple_of(start, NX), NX)


def substep_kernel(src, kap, rates, dst):
    lane = lax.broadcasted_iota(jnp.int32, (NX, 128), 1)

    def body(z, others):
        halves = [[src[g, h, plane_at(z), :] for g in range(NF)] for h in range(2)]
        for f in range(NF):
            k = kap[f]
            a, b = halves[0][f], halves[1][f]
            a_up, b_up = pltpu.roll(a, 1, 1), pltpu.roll(b, 1, 1)
            a_down, b_down = pltpu.roll(a, 127, 1), pltpu.roll(b, 127, 1)
            sides = (
                jnp.where(lane == 0, b_up, a_up) + jnp.where(lane == 127, b_down, a_down),
                jnp.where(lane == 0, a_up, b_up) + jnp.where(lane == 127, a_down, b_down),
            )
            for h in range(2):
                v = halves[h][f]
                near = pltpu.roll(v, 1, 0) + pltpu.roll(v, NX - 1, 0) + sides[h]
                for other in others:
                    near = near + src[f, h, plane_at(other), :]
                dst[f, h, plane_at(z), :] = (
                    reacted(halves[h], f, 0.5, 1.0 - 12.0 * k, rates) + (2.0 * k) * near
                )

    body(0, (1,))

    def step(z, carry):
        body(z, (z - 1, z + 1))
        return carry

    lax.fori_loop(1, NZ - 1, step, 0)
    body(NZ - 1, (NZ - 2,))


def add_ghost(dst, z, tiles, kap):
    wide = table_dot(jnp.concatenate(tiles, axis=0), spread_table())
    for f in range(NF):
        part = (2.0 * kap[f]) * wide[f * 8 : f * 8 + 8]
        for h in range(2):
            for x in range(2):
                rows = pl.ds(z * NX + x, 8, stride=2)
                dst[f, h, rows, :] = dst[f, h, rows, :] + part[:, h * 128 : (h + 1) * 128]


def is_even(axis):
    return (lax.axis_index(axis) & 1) == 0


def pick(flag, one, other):
    return jnp.where(flag, one, other)


def prep_kernel(c, u_in, u, odd, even, own, packs, sems):
    even_y = is_even("gy")
    copies = [
        pltpu.make_async_copy(u_in.at[:, :, h * 128 : (h + 1) * 128], u.at[:, h], sems.at[h])
        for h in range(2)
    ]
    for n, (slot, dst) in enumerate(((pick(even_y, 0, 2), odd), (pick(even_y, 2, 0), even), (1, own))):
        for side, k in ((0, LOW), (1, HIGH)):
            copies.append(
                pltpu.make_async_copy(
                    c.at[slot, :, k], dst.at[pl.ds(side * NF, NF)], sems.at[2 + 2 * n + side]
                )
            )
    for copy in copies:
        copy.start()
    for copy in copies[:2]:
        copy.wait()
    packed = [pack_columns(u, side) for side in range(2)]
    for t in range(2):
        left, right = (packed[side][8 * t : 8 * t + 8] for side in range(2))
        packs[t] = left
        packs[2 + t] = right
        odd[18 + t] = pick(even_y, left, right)
        even[18 + t] = pick(even_y, right, left)
    for copy in copies[2:]:
        copy.wait()


def middle_kernel(c, kap, rates, odd, even, own):
    even_y = is_even("gy")
    for slot, dst in ((pick(even_y, 0, 2), odd), (1, own), (pick(even_y, 2, 0), even)):
        for side, k in ((0, LOW), (1, HIGH)):
            tiles = [c[slot, g, k] for g in range(NF)]
            for f in range(NF):
                kf = kap[f]
                near = c[slot, f, k - 1] + c[slot, f, k + 1]
                dst[side * NF + f] = (
                    reacted(tiles, f, 0.5, 1.0 - kf, rates) + (0.5 * kf) * near
                )


def chosen(owner, odd, even, own, rims):
    mine = owner[lax.axis_index("gx"), lax.axis_index("gy")]
    at_odd = mine == pick(is_even("gy"), -1, 1)
    for t in range(18):
        rims[t] = jnp.where(mine == 0, own[t], jnp.where(at_odd, odd[t], even[t]))


def stacked(ref, at):
    return jnp.concatenate([ref[at], ref[at + 1]], axis=0)


def first_kernel(
    u, w, odd_in, even_in, own, packs, y_odd_in, y_even_in, owner, kap,
    u1, y_odd, y_even, x_odd, x_even, rims, packs1,
):
    even_y = is_even("gy")
    even_x = is_even("gx")
    chosen(owner, odd_in, even_in, own, rims)
    add_ghost(u1, 0, [rims[f] for f in range(NF)], kap)
    add_ghost(u1, NZ - 1, [rims[NF + f] for f in range(NF)], kap)
    k_lanes = kappa_lanes(kap)
    odd, even = stacked(odd_in, 18), stacked(even_in, 18)
    from_left = pick(even_y, odd, even)
    from_right = pick(even_y, even, odd)
    left = k_lanes * (from_left - stacked(packs, 2))
    right = k_lanes * (from_right - stacked(packs, 0))
    add_columns(u1, left, right)
    for f in range(NF):
        k2 = 2.0 * kap[f]
        for h in range(2):
            first = row_of(u, f, h, 0)
            last = row_of(u, f, h, NX - 1)
            new_first = row_of(u1, f, h, 0) - k2 * last
            new_last = row_of(u1, f, h, NX - 1) - k2 * first
            set_row(u1, f, h, 0, new_first)
            set_row(u1, f, h, NX - 1, new_last)
            x_odd[2 * f + h] = pick(even_x, first, last)
            x_odd[18 + 2 * f + h] = pick(even_x, new_first, new_last)
            x_even[2 * f + h] = pick(even_x, last, first)
            x_even[18 + 2 * f + h] = pick(even_x, new_last, new_first)
    facing = (from_left, from_right, stacked(packs, 0), stacked(packs, 2))
    for n, value in enumerate(facing):
        x_odd[36 + n] = pick(even_x, value[0:8], value[8:16])
        x_even[36 + n] = pick(even_x, value[8:16], value[0:8])
    packed = [pack_columns(u1, side) for side in range(2)]
    for t in range(2):
        left, right = (packed[side][8 * t : 8 * t + 8] for side in range(2))
        packs1[t] = left
        packs1[2 + t] = right
        y_odd[18 + t] = pick(even_y, left, right)
        y_even[18 + t] = pick(even_y, right, left)


def pair_rows(ref, f, half, z):
    return (
        ref[f, half, pl.ds(z * NX, 8, stride=2), :]
        + ref[f, half, pl.ds(z * NX + 1, 8, stride=2), :]
    )


def add_rows(u, u1, new, message, k_of, rates, first):
    here = pick(first, 0, NX - 1)
    inner = pick(first, 1, NX - 2)
    opposite = pick(first, NX - 1, 0)
    layer = lax.broadcasted_iota(jnp.int32, (NZ, 128), 0)
    lane = lax.broadcasted_iota(jnp.int32, (NZ, 128), 1)
    delta = [[2.0 * k_of(g) * message[2 * g + h] for g in range(NF)] for h in range(2)]
    for f in range(NF):
        k = k_of(f)
        k2 = 2.0 * k
        a, b = delta[0][f], delta[1][f]
        a_up, b_up = pltpu.roll(a, 1, 1), pltpu.roll(b, 1, 1)
        a_down, b_down = pltpu.roll(a, 127, 1), pltpu.roll(b, 127, 1)
        sides = (
            jnp.where(lane == 0, b_up, a_up) + jnp.where(lane == 127, b_down, a_down),
            jnp.where(lane == 0, a_up, b_up) + jnp.where(lane == 127, a_down, b_down),
        )
        for h in range(2):
            d = delta[h][f]
            near = sides[h] + jnp.where(layer == 0, 0.0, pltpu.roll(d, 1, 0))
            near = near + jnp.where(layer == NZ - 1, 0.0, pltpu.roll(d, NZ - 1, 0))
            halo = message[18 + 2 * f + h] + k2 * row_of(u, f, h, here)
            near = near + (halo - row_of(u1, f, h, opposite))
            more = reacted(delta[h], f, 0.5, 1.0 - 12.0 * k, rates) + k2 * near
            set_row(new, f, h, here, row_of(new, f, h, here) + more)
            set_row(new, f, h, inner, row_of(new, f, h, inner) + k2 * d)
    return delta


def second_kernel(
    u, u1, new_in, x_odd, x_even, y_odd, y_even, own_mid, packs1, old, owner, kap, rates,
    new, payload, mids, sums,
):
    even_y = is_even("gy")
    even_x = is_even("gx")
    chosen(owner, y_odd, y_even, own_mid, mids)
    add_ghost(new, 0, [mids[f] for f in range(NF)], kap)
    add_ghost(new, NZ - 1, [mids[NF + f] for f in range(NF)], kap)
    k_of = lambda f: kap[f]
    delta_odd = add_rows(u, u1, new, x_odd, k_of, rates, even_x)
    delta_even = add_rows(u, u1, new, x_even, k_of, rates, jnp.logical_not(even_x))
    k_lanes = kappa_lanes(kap)
    x_id = lax.broadcasted_iota(jnp.int32, (NX, 128), 0)

    def facing(tile):
        low = pltpu.roll(pick(even_x, x_odd[tile], x_even[tile]), 1, 0)
        high = pltpu.roll(pick(even_x, x_even[tile], x_odd[tile]), 7, 0)
        both = jnp.concatenate([low, high], axis=0)
        return k_lanes * jnp.where((x_id == 0) | (x_id == NX - 1), both, 0.0)

    odd, even = stacked(y_odd, 18), stacked(y_even, 18)
    left = pick(even_y, odd, even) + facing(36) - (stacked(packs1, 2) + facing(39))
    right = pick(even_y, even, odd) + facing(37) - (stacked(packs1, 0) + facing(38))
    add_columns(new, k_lanes * left, k_lanes * right)
    row_odd = pick(even_x, 0, 7)
    row_even = pick(even_x, 7, 0)
    row_id = lax.broadcasted_iota(jnp.int32, (8, 128), 0)
    for f in range(NF):
        for h in range(2):
            lanes = slice(h * 128, (h + 1) * 128)
            for c in range(4):
                sums[f * 6 + 1 + c, :, lanes] = pair_rows(new, f, h, 2 * c) + pair_rows(
                    new, f, h, 2 * c + 1
                )
            for at, z in ((0, 0), (5, NZ - 1)):
                pair = pair_rows(u, f, h, z) + pair_rows(u1, f, h, z)
                odd = delta_odd[h][f][z : z + 1]
                even = delta_even[h][f][z : z + 1]
                pair = pair + jnp.where(
                    row_id == row_odd, odd, jnp.where(row_id == row_even, even, 0.0)
                )
                sums[f * 6 + at, :, lanes] = pair
    table = gather_table()
    for f in range(NF):
        coarse = table_dot(sums[f * 6 : f * 6 + 6].reshape(48, NY), table)
        for c in range(4):
            payload[f * 6 + 1 + c] = coarse[8 + c * 8 : c * 8 + 16] * 0.125
        kf = kap[f]
        payload[f * 6] = kf * (old[f] + mids[f] - 0.25 * coarse[0:8])
        payload[f * 6 + 5] = kf * (0.25 * coarse[40:48] - old[9 + f] - mids[9 + f])


def used_flags(owner):
    row = lax.axis_index("gx")
    col = lax.axis_index("gy")
    size = lax.axis_size("gy")
    left = owner[row, lax.rem(col + size - 1, size)] == 1
    self_used = owner[row, col] == 0
    right = owner[row, lax.rem(col + 1, size)] == -1
    return left, self_used, right


def coarse_kernel(c, new, payload, owner, kap, rates, out, fine_out, base, full, sems):
    copies = [
        pltpu.make_async_copy(new.at[:, h], fine_out.at[:, :, h * 128 : (h + 1) * 128], sems.at[h])
        for h in range(2)
    ]
    for copy in copies:
        copy.start()
    for slot, used in enumerate(used_flags(owner)):
        for k in (0, 1, 2, 3, 8, 9, 10, 11):
            tiles = [c[slot, g, k] for g in range(NF)]
            for f in range(NF):
                kf = kap[f]
                near = None
                count = 0.0
                if k not in (0, HIGH):
                    near = c[slot, f, k - 1]
                    count += 1.0
                if k not in (LOW, 11):
                    above = c[slot, f, k + 1]
                    near = above if near is None else near + above
                    count += 1.0
                value = reacted(tiles, f, 1.0, 1.0 - count * kf, rates) + kf * near
                if k == LOW:
                    base[slot, f, 0] = value
                    if slot == 1:
                        value = value - payload[f * 6]
                if k == HIGH:
                    base[slot, f, 1] = value
                    if slot == 1:
                        value = value + payload[f * 6 + 5]
                full[slot, f, k] = jnp.where(used, value, tiles[f])
        for f in range(NF):
            for k in range(4, 8):
                value = c[slot, f, k]
                if slot == 1:
                    value = jnp.where(used, payload[f * 6 + k - 3], value)
                full[slot, f, k] = value
        copy = pltpu.make_async_copy(full.at[slot], out.at[slot], sems.at[2 + slot])
        copy.start()
        copies.append(copy)
    for copy in copies:
        copy.wait()


def finish_kernel(out_in, base, odd, even, owner, out, fixed, sems):
    flags = used_flags(owner)
    even_y = is_even("gy")
    for n, slot in enumerate((0, 2)):
        at_odd = even_y if slot == 0 else jnp.logical_not(even_y)
        for src, here in ((odd, at_odd), (even, jnp.logical_not(at_odd))):

            @pl.when(jnp.logical_and(flags[slot], here))
            def _(n=n, slot=slot, src=src):
                for f in range(NF):
                    fixed[n, f, 0] = base[slot, f, 0] - src[f, 0]
                    for k in range(1, 5):
                        fixed[n, f, k] = src[f, k]
                    fixed[n, f, 5] = base[slot, f, 1] + src[f, 5]
                pltpu.make_async_copy(
                    fixed.at[n], out.at[slot, :, LOW : HIGH + 1], sems.at[n]
                ).start()

    for n, slot in enumerate((0, 2)):

        @pl.when(flags[slot])
        def _(n=n, slot=slot):
            pltpu.make_async_copy(fixed.at[n], out.at[slot, :, LOW : HIGH + 1], sems.at[n]).wait()


def swapped(value, axis, odd):
    size = lax.axis_size(axis)
    pairs = []
    for i in range(odd, size, 2):
        j = (i + 1) % size
        pairs += [(i, j), (j, i)]
    return lax.ppermute(value, axis, pairs)


def both(odd, even, axis):
    return swapped(odd, axis, 1), swapped(even, axis, 0)


def on_device(fine_state, coarse_column_state, diffusivity, rates, owner_offset):
    fine_shape = fine_state.shape
    u_in = fine_state.reshape(NF, NZ * NX, NY)
    c = coarse_column_state
    split = (NF, 2, NZ * NX, 128)
    dma = pltpu.SemaphoreType.DMA
    u, odd, even, own, packs = call(
        prep_kernel,
        "prep",
        [split, (20, 8, 128), (20, 8, 128), (18, 8, 128), (4, 8, 128)],
        [pltpu.HBM, pltpu.HBM],
        1 << 20,
        limit=58,
        scratch=[dma((8,))],
    )(c, u_in)
    odd, even = both(odd, even, "gy")
    y_odd, y_even, own_mid = call(
        middle_kernel,
        "middle",
        [(20, 8, 128), (20, 8, 128), (18, 8, 128)],
        [VMEM, SMEM, SMEM],
        1 << 25,
    )(c, diffusivity, rates)

    def substep(v, name):
        (w,) = call(substep_kernel, name, [split], [VMEM, SMEM, SMEM], 1 << 27)(
            v, diffusivity, rates
        )
        return w

    w = substep(u, "inner1")
    u1, y_odd, y_even, x_odd, x_even, old, packs1 = call(
        first_kernel,
        "first",
        [split, (20, 8, 128), (20, 8, 128), (40, 8, 128), (40, 8, 128), (18, 8, 128), (4, 8, 128)],
        [VMEM] * 8 + [SMEM] * 2,
        1 << 26,
        aliases={1: 0, 6: 1, 7: 2},
    )(u, w, odd, even, own, packs, y_odd, y_even, owner_offset, diffusivity)
    x_odd, x_even = both(x_odd, x_even, "gx")
    y_odd, y_even = both(y_odd, y_even, "gy")
    w = substep(u1, "inner2")
    new, payload = call(
        second_kernel,
        "second",
        [split, (54, 8, 128)],
        [VMEM] * 10 + [SMEM] * 3,
        1 << 26,
        aliases={2: 0},
        scratch=[pltpu.VMEM((18, 8, 128), F32), pltpu.VMEM((54, 8, NY), F32)],
    )(
        u, u1, w, x_odd, x_even, y_odd, y_even, own_mid, packs1, old, owner_offset,
        diffusivity, rates,
    )
    odd, even = both(payload, payload, "gy")
    out, fine_new, base = call(
        coarse_kernel,
        "coarse",
        [c.shape, u_in.shape, (3, NF, 2, 8, 128)],
        [VMEM] * 3 + [SMEM] * 3,
        1 << 26,
        scratch=[pltpu.VMEM(c.shape, F32), dma((5,))],
        out_spaces=[pltpu.HBM, pltpu.HBM, VMEM],
    )(c, new, payload, owner_offset, diffusivity, rates)
    six = (NF, 6, 8, 128)
    (coarse_new,) = call(
        finish_kernel,
        "finish",
        [c.shape],
        [pltpu.HBM, VMEM, VMEM, VMEM, SMEM],
        1 << 20,
        aliases={0: 0},
        scratch=[pltpu.VMEM((2,) + six, F32), dma((2,))],
        out_spaces=[pltpu.HBM],
    )(out, base, odd.reshape(six), even.reshape(six), owner_offset)
    return fine_new.reshape(fine_shape), coarse_new


def solution(mesh):
    in_specs = (P(None, None, "gx", "gy"), P(None, None, None, "gx", "gy"), P(), P(), P())
    out_specs = (P(None, None, "gx", "gy"), P(None, None, None, "gx", "gy"))
    return jax.shard_map(
        on_device, mesh=mesh, in_specs=in_specs, out_specs=out_specs, check_vma=False
    )
```

```python
import jax
import jax.numpy as jnp
from jax import lax
from jax.experimental import pallas as pl
from jax.experimental.pallas import tpu as pltpu
from jax.sharding import PartitionSpec as P


F32 = jnp.float32
BF16 = jnp.bfloat16
NF = 9
NZ = 8
NX = 16
NY = 256
LOW = 3
HIGH = 8
VMEM = pltpu.VMEM
SMEM = pltpu.SMEM


def call(kernel, outs, spaces, flops, limit=8, aliases=None, scratch=(), out_spaces=None):
    return pl.pallas_call(
        kernel,
        out_shape=[jax.ShapeDtypeStruct(s, F32) for s in outs],
        in_specs=[pl.BlockSpec(memory_space=s) for s in spaces],
        out_specs=[pl.BlockSpec(memory_space=s) for s in out_spaces or [VMEM] * len(outs)],
        scratch_shapes=list(scratch),
        input_output_aliases=aliases or {},
        compiler_params=pltpu.CompilerParams(vmem_limit_bytes=int(limit * (1 << 20))),
        cost_estimate=pl.CostEstimate(flops=flops, bytes_accessed=1 << 20, transcendentals=0),
    )


def spread_table():
    coarse = lax.broadcasted_iota(jnp.int32, (128, 256), 0)
    fine = lax.broadcasted_iota(jnp.int32, (128, 256), 1)
    return jnp.where(lax.shift_right_logical(fine, 1) == coarse, 1.0, 0.0).astype(BF16)


def gather_table():
    fine = lax.broadcasted_iota(jnp.int32, (256, 128), 0)
    coarse = lax.broadcasted_iota(jnp.int32, (256, 128), 1)
    return jnp.where(lax.shift_right_logical(fine, 1) == coarse, 1.0, 0.0).astype(BF16)


def table_dot(value, table):
    high = value.astype(BF16)
    low = (value - high.astype(F32)).astype(BF16)
    return jnp.dot(high, table, preferred_element_type=F32) + jnp.dot(
        low, table, preferred_element_type=F32
    )


def reacted(tiles, f, scale, diagonal, rates):
    total = tiles[f] * (diagonal + scale * rates[f, f])
    for g in range(NF):
        if g != f:
            total = total + tiles[g] * (scale * rates[f, g])
    return total


def pack_columns(plane_of, side, fields=range(NF), packed=None):
    lane = lax.broadcasted_iota(jnp.int32, (NX, 128), 1)
    if packed is None:
        packed = jnp.zeros((NX, 128), F32)
    for f in fields:
        for z in range(NZ):
            at = z * 16 + f
            shift = at if side == 0 else (at - 127) % 128
            tile = plane_of(f, side, z)
            moved = pltpu.roll(tile, shift, 1) if shift else tile
            packed = jnp.where(lane == at, moved, packed)
    return packed


def split_plane(ref):
    return lambda f, h, z: ref[f, h, z * NX : (z + 1) * NX, :]


def whole_plane(ref):
    return lambda f, h, z: ref[f, z * NX : (z + 1) * NX, h * 128 : (h + 1) * 128]


def put_packs(packs, packed):
    for side in range(2):
        for t in range(2):
            packs[2 * side + t] = packed[side][8 * t : 8 * t + 8]


def kappa_lanes(kap):
    lane = lax.broadcasted_iota(jnp.int32, (NX, 128), 1) & 15
    out = jnp.zeros((NX, 128), F32)
    for f in range(NF):
        out = jnp.where(lane == f, 2.0 * kap[f], out)
    return out


def add_columns(ref, left, right):
    lane = lax.broadcasted_iota(jnp.int32, (NX, 128), 1)
    for z in range(NZ):
        rows = slice(z * NX, (z + 1) * NX)
        for f in range(NF):
            at = z * 16 + f
            moved = pltpu.roll(left, 128 - at, 1) if at else left
            ref[f, 0, rows, :] = ref[f, 0, rows, :] + jnp.where(lane == 0, moved, 0.0)
            shift = 127 - at
            moved = pltpu.roll(right, shift, 1) if shift else right
            ref[f, 1, rows, :] = ref[f, 1, rows, :] + jnp.where(lane == 127, moved, 0.0)


def row_of(ref, f, half, row):
    return ref[f, half, pl.ds(row, NZ, stride=NX), :]


def set_row(ref, f, half, row, value):
    ref[f, half, pl.ds(row, NZ, stride=NX), :] = value


def plane_at(z):
    start = z * NX
    return pl.ds(start if isinstance(z, int) else pl.multiple_of(start, NX), NX)


def substep(src, dst, mixed, k2, copy=None):
    lane = lax.broadcasted_iota(jnp.int32, (NX, 128), 1)

    def tile(f, h, z):
        if copy is None:
            return src[f, h, plane_at(z), :]
        return src[f, plane_at(z), h * 128 : (h + 1) * 128]

    def body(z, others):
        halves = [[tile(g, h, z) for g in range(NF)] for h in range(2)]
        for f in range(NF):
            a, b = halves[0][f], halves[1][f]
            a_up, b_up = pltpu.roll(a, 1, 1), pltpu.roll(b, 1, 1)
            a_down, b_down = pltpu.roll(a, 127, 1), pltpu.roll(b, 127, 1)
            sides = (
                jnp.where(lane == 0, b_up, a_up) + jnp.where(lane == 127, b_down, a_down),
                jnp.where(lane == 0, a_up, b_up) + jnp.where(lane == 127, a_down, b_down),
            )
            for h in range(2):
                v = halves[h][f]
                if copy is not None:
                    copy[f, h, plane_at(z), :] = v
                near = pltpu.roll(v, 1, 0) + pltpu.roll(v, NX - 1, 0) + sides[h]
                for other in others:
                    near = near + tile(f, h, other)
                dst[f, h, plane_at(z), :] = mixed(halves[h], f) + k2(f) * near

    body(0, (1,))

    def step(z, carry):
        body(z, (z - 1, z + 1))
        return carry

    lax.fori_loop(1, NZ - 1, step, 0)
    body(NZ - 1, (NZ - 2,))


def add_ghost(dst, z, tiles, kap):
    wide = table_dot(jnp.concatenate(tiles, axis=0), spread_table())
    for f in range(NF):
        for h in range(2):
            part = (2.0 * kap[f]) * wide[f * 8 : f * 8 + 8, h * 128 : (h + 1) * 128]
            for x in range(2):
                rows = pl.ds(z * NX + x, 8, stride=2)
                dst[f, h, rows, :] = dst[f, h, rows, :] + part


def is_even(axis):
    return (lax.axis_index(axis) & 1) == 0


def pick(flag, one, other):
    return jnp.where(flag, one, other)


def prep_kernel(c, u_in, u, odd, even, own, packs, sems):
    even_y = is_even("gy")
    fine = [
        pltpu.make_async_copy(u_in.at[3 * n : 3 * n + 3], u.at[3 * n : 3 * n + 3], sems.at[n])
        for n in range(3)
    ]
    copies = []
    for n, (slot, dst) in enumerate(((pick(even_y, 0, 2), odd), (pick(even_y, 2, 0), even), (1, own))):
        for side, k in ((0, LOW), (1, HIGH)):
            copies.append(
                pltpu.make_async_copy(
                    c.at[slot, :, k], dst.at[pl.ds(side * NF, NF)], sems.at[3 + 2 * n + side]
                )
            )
    for copy in fine + copies:
        copy.start()
    packed = [None, None]
    for n, copy in enumerate(fine):
        copy.wait()
        packed = [
            pack_columns(whole_plane(u), side, range(3 * n, 3 * n + 3), packed[side])
            for side in range(2)
        ]
    put_packs(packs, packed)
    for t in range(2):
        left, right = (packed[side][8 * t : 8 * t + 8] for side in range(2))
        odd[18 + t] = pick(even_y, left, right)
        even[18 + t] = pick(even_y, right, left)
    for copy in copies:
        copy.wait()


def pair_rows(ref, f, half, z):
    return (
        ref[f, half, pl.ds(z * NX, 8, stride=2), :]
        + ref[f, half, pl.ds(z * NX + 1, 8, stride=2), :]
    )


def tall(tile):
    return jnp.concatenate([tile, tile], axis=0)


class Shared:
    count = 95

    def __init__(self, ref):
        self.ref = ref

    def __getitem__(self, f):
        return self.ref[81 + f]

    def lanes(self):
        return self.ref[90]

    def flag(self, n):
        return self.ref[91 + n] > 0.5

    def mixed(self, tiles, f):
        total = tiles[0] * self.ref[f * NF]
        for g in range(1, NF):
            total = total + tiles[g] * self.ref[f * NF + g]
        return total

    def mixed_tall(self, tiles, f):
        total = tiles[0] * tall(self.ref[f * NF])
        for g in range(1, NF):
            total = total + tiles[g] * tall(self.ref[f * NF + g])
        return total


def fill_shared(shared, owner, kap, rates):
    for f in range(NF):
        for g in range(NF):
            value = 0.5 * rates[f, g]
            if f == g:
                value = value + (1.0 - 12.0 * kap[f])
            shared[f * NF + g] = jnp.full((8, 128), value, F32)
        shared[81 + f] = jnp.full((8, 128), kap[f], F32)
    shared[90] = kappa_lanes(kap)[0:8]
    mine = owner[lax.axis_index("gx"), lax.axis_index("gy")]
    left, _, right = used_flags(owner)
    flags = (mine == 0, mine == pick(is_even("gy"), -1, 1), left, right)
    for n, flag in enumerate(flags):
        shared[91 + n] = jnp.full((8, 128), jnp.where(flag, 1.0, 0.0), F32)


def inner1_kernel(
    u_in, c, kap, rates, owner, w, u, packs, sums, odd, even, own, shared, pairs
):
    fill_shared(shared, owner, kap, rates)
    substep(
        u_in,
        w,
        lambda tiles, f: reacted(tiles, f, 0.5, 1.0 - 12.0 * kap[f], rates),
        lambda f: 2.0 * kap[f],
        u,
    )
    for f in range(NF):
        k2 = 2.0 * kap[f]
        for h in range(2):
            set_row(w, f, h, 0, row_of(w, f, h, 0) - k2 * row_of(u, f, h, NX - 1))
            set_row(w, f, h, NX - 1, row_of(w, f, h, NX - 1) - k2 * row_of(u, f, h, 0))
    put_packs(packs, [pack_columns(split_plane(w), side) for side in range(2)])
    for side, z in ((0, 0), (1, NZ - 1)):
        for f in range(NF):
            for h in range(2):
                pairs[side * NF + f, :, h * 128 : (h + 1) * 128] = pair_rows(u, f, h, z) + pair_rows(
                    w, f, h, z
                )
    coarse = table_dot(pairs[...].reshape(18 * 8, NY), gather_table())
    for t in range(18):
        sums[t] = 0.25 * coarse[t * 8 : t * 8 + 8]
    even_y = is_even("gy")
    for slot, dst in ((pick(even_y, 0, 2), odd), (1, own), (pick(even_y, 2, 0), even)):
        for side, k in ((0, LOW), (1, HIGH)):
            tiles = [c[slot, g, k] for g in range(NF)]
            for f in range(NF):
                kf = kap[f]
                near = c[slot, f, k - 1] + c[slot, f, k + 1]
                dst[side * NF + f] = (
                    reacted(tiles, f, 0.5, 1.0 - kf, rates) + (0.5 * kf) * near
                )


def chosen(shared, odd, even, own, rims):
    at_own = shared.flag(0)
    at_odd = shared.flag(1)
    for t in range(18):
        rims[t] = jnp.where(at_own, own[t], jnp.where(at_odd, odd[t], even[t]))


def stacked(ref, at):
    return jnp.concatenate([ref[at], ref[at + 1]], axis=0)


def refined(tiles):
    return table_dot(jnp.concatenate(tiles, axis=0), spread_table())


def edges_kernel(
    u, w, odd_in, even_in, own, packs, packs_w, sums_w, y_odd_in, y_even_in, shared,
    y_odd, y_even, x_odd, x_even, rims, packs1, columns, sums, ghost,
):
    even_y = is_even("gy")
    even_x = is_even("gx")
    kap = Shared(shared)
    chosen(kap, odd_in, even_in, own, rims)
    k_lanes = tall(kap.lanes())
    odd, even = stacked(odd_in, 18), stacked(even_in, 18)
    from_left = pick(even_y, odd, even)
    from_right = pick(even_y, even, odd)
    left = k_lanes * (from_left - stacked(packs, 2))
    right = k_lanes * (from_right - stacked(packs, 0))
    put_packs(columns, [left, right])
    lane = lax.broadcasted_iota(jnp.int32, (8, 128), 1)
    for side in range(2):
        packed = jnp.zeros((8, 128), F32)
        for f in range(NF):
            for at, tile in ((f, rims[f]), (112 + f, rims[NF + f])):
                shift = at if side == 0 else (at - 127) % 128
                moved = pltpu.roll(tile, shift, 1) if shift else tile
                packed = jnp.where(lane == at, moved, packed)
        packed = packed * k_lanes[0:8]
        ghost[side, pl.ds(0, 8, stride=2), :] = packed
        ghost[side, pl.ds(1, 8, stride=2), :] = packed
    new_left = stacked(packs_w, 0) + left + ghost[0]
    new_right = stacked(packs_w, 2) + right + ghost[1]
    put_packs(packs1, [new_left, new_right])
    for t in range(2):
        a, b = new_left[8 * t : 8 * t + 8], new_right[8 * t : 8 * t + 8]
        y_odd[18 + t] = pick(even_y, a, b)
        y_even[18 + t] = pick(even_y, b, a)
    totals = []
    for side, value in enumerate((left, right)):
        ghost[side] = value
        totals.append(
            0.25 * (ghost[side, pl.ds(0, 8, stride=2), :] + ghost[side, pl.ds(1, 8, stride=2), :])
        )
    for side in range(2):
        for f in range(NF):
            kf = kap[f]
            at = 112 * side + f
            a = pltpu.roll(totals[0], 128 - at, 1) if at else totals[0]
            b = pltpu.roll(totals[1], 127 - at, 1)
            t = side * NF + f
            flux = sums_w[t] + jnp.where(lane == 0, a, jnp.where(lane == 127, b, 0.0))
            flux = flux + (2.0 * kf - 1.0) * rims[t]
            value = (-kf if side == 0 else kf) * flux
            sums[t] = value
            y_odd[20 + t] = value
            y_even[20 + t] = value
    wide_low = refined([rims[f] for f in range(NF)])
    wide_high = refined([rims[NF + f] for f in range(NF)])
    layer = lax.broadcasted_iota(jnp.int32, (NZ, 128), 0)
    for f in range(NF):
        k2 = 2.0 * kap[f]
        for h in range(2):
            lanes = slice(h * 128, (h + 1) * 128)
            first = row_of(u, f, h, 0)
            last = row_of(u, f, h, NX - 1)
            values = []
            for row, at in ((0, f * 8), (NX - 1, f * 8 + 7)):
                more = jnp.where(
                    layer == 0,
                    wide_low[at : at + 1, lanes],
                    jnp.where(layer == NZ - 1, wide_high[at : at + 1, lanes], 0.0),
                )
                values.append(row_of(w, f, h, row) + k2 * more)
            x_odd[2 * f + h] = pick(even_x, first, last)
            x_odd[18 + 2 * f + h] = pick(even_x, values[0], values[1])
            x_even[2 * f + h] = pick(even_x, last, first)
            x_even[18 + 2 * f + h] = pick(even_x, values[1], values[0])
    facing = (from_left, from_right, stacked(packs, 0), stacked(packs, 2))
    for n, value in enumerate(facing):
        x_odd[36 + n] = pick(even_x, value[0:8], value[8:16])
        x_even[36 + n] = pick(even_x, value[8:16], value[0:8])


def inner2_kernel(w, rims, columns, shared, u1, new, averages, sums):
    kap = Shared(shared)
    add_ghost(u1, 0, [rims[f] for f in range(NF)], kap)
    add_ghost(u1, NZ - 1, [rims[NF + f] for f in range(NF)], kap)
    add_columns(u1, stacked(columns, 0), stacked(columns, 2))
    substep(u1, new, kap.mixed_tall, lambda f: tall(2.0 * kap[f]))
    for f in range(NF):
        for h in range(2):
            lanes = slice(h * 128, (h + 1) * 128)
            for c in range(4):
                sums[f * 4 + c, :, lanes] = pair_rows(new, f, h, 2 * c) + pair_rows(
                    new, f, h, 2 * c + 1
                )
    table = gather_table()
    for f in range(NF):
        coarse = table_dot(sums[f * 4 : f * 4 + 4].reshape(32, NY), table)
        for c in range(4):
            averages[f * 4 + c] = coarse[c * 8 : c * 8 + 8] * 0.125


def row_terms(u, u1, message, kap, first, deltas, mores):
    here = pick(first, 0, NX - 1)
    opposite = pick(first, NX - 1, 0)
    layer = lax.broadcasted_iota(jnp.int32, (NZ, 128), 0)
    lane = lax.broadcasted_iota(jnp.int32, (NZ, 128), 1)
    delta = [[2.0 * kap[g] * message[2 * g + h] for g in range(NF)] for h in range(2)]
    for f in range(NF):
        k = kap[f]
        k2 = 2.0 * k
        a, b = delta[0][f], delta[1][f]
        a_up, b_up = pltpu.roll(a, 1, 1), pltpu.roll(b, 1, 1)
        a_down, b_down = pltpu.roll(a, 127, 1), pltpu.roll(b, 127, 1)
        sides = (
            jnp.where(lane == 0, b_up, a_up) + jnp.where(lane == 127, b_down, a_down),
            jnp.where(lane == 0, a_up, b_up) + jnp.where(lane == 127, a_down, b_down),
        )
        for h in range(2):
            d = delta[h][f]
            near = sides[h] + jnp.where(layer == 0, 0.0, pltpu.roll(d, 1, 0))
            near = near + jnp.where(layer == NZ - 1, 0.0, pltpu.roll(d, NZ - 1, 0))
            halo = message[18 + 2 * f + h] + k2 * row_of(u, f, h, here)
            near = near + (halo - row_of(u1, f, h, opposite))
            more = kap.mixed(delta[h], f) + k2 * near
            deltas[2 * f + h] = k2 * d
            mores[2 * f + h] = more
    return delta


def payload_kernel(
    u, u1, averages, x_odd, x_even, y_odd, y_even, own_mid, packs1, shared,
    payload, mids, deltas, mores, columns, pairs, rows,
):
    even_y = is_even("gy")
    even_x = is_even("gx")
    kap = Shared(shared)
    chosen(kap, y_odd, y_even, own_mid, mids)
    row_odd = pick(even_x, 0, 7)
    row_even = pick(even_x, 7, 0)
    for n, (message, first) in enumerate(((x_odd, even_x), (x_even, jnp.logical_not(even_x)))):
        delta = row_terms(u, u1, message, kap, first, deltas.at[n], mores.at[n])
        for f in range(NF):
            for h in range(2):
                lanes = slice(h * 128, (h + 1) * 128)
                rows[n, f, :, lanes] = mores[n, 2 * f + h] + deltas[n, 2 * f + h]
                rows[2 + n, f, :, lanes] = delta[h][f]
    table = gather_table()
    coarse = table_dot(rows[...].reshape(4 * NF * NZ, NY), table).reshape(4, NF, NZ, 128)
    k_lanes = tall(kap.lanes())
    x_id = lax.broadcasted_iota(jnp.int32, (NX, 128), 0)

    def facing(tile):
        low = pltpu.roll(pick(even_x, x_odd[tile], x_even[tile]), 1, 0)
        high = pltpu.roll(pick(even_x, x_even[tile], x_odd[tile]), 7, 0)
        both = jnp.concatenate([low, high], axis=0)
        return k_lanes * jnp.where((x_id == 0) | (x_id == NX - 1), both, 0.0)

    odd, even = stacked(y_odd, 18), stacked(y_even, 18)
    left = pick(even_y, odd, even) - stacked(packs1, 2) + 2.0 * (facing(36) - facing(39))
    right = pick(even_y, even, odd) - stacked(packs1, 0) + 2.0 * (facing(37) - facing(38))
    left = k_lanes * left
    right = k_lanes * right
    put_packs(columns, [left, right])
    side_sums = []
    for n, value in enumerate((left, right)):
        pairs[n] = value
        total = pairs[n, pl.ds(0, 8, stride=2), :] + pairs[n, pl.ds(1, 8, stride=2), :]
        side_sums.append(0.125 * (total + pltpu.roll(total, 112, 1)))
    row_id = lax.broadcasted_iota(jnp.int32, (8, 128), 0)
    lane = lax.broadcasted_iota(jnp.int32, (8, 128), 1)
    at_odd = row_id == row_odd
    at_even = row_id == row_even
    for f in range(NF):
        kf = kap[f]
        halves = [0.125 * (coarse[n, f] + pltpu.roll(coarse[n, f], NZ - 1, 0)) for n in range(2)]
        for c in range(4):
            value = averages[f * 4 + c]
            if c == 0:
                value = value + kf * mids[f]
            if c == 3:
                value = value + kf * mids[NF + f]
            z = 2 * c
            value = value + jnp.where(
                at_odd, halves[0][z : z + 1], jnp.where(at_even, halves[1][z : z + 1], 0.0)
            )
            at = z * 16 + f
            a = pltpu.roll(side_sums[0], 128 - at, 1) if at else side_sums[0]
            b = pltpu.roll(side_sums[1], 127 - at, 1) if at != 127 else side_sums[1]
            value = value + jnp.where(lane == 0, a, jnp.where(lane == 127, b, 0.0))
            payload[f * 4 + c] = value
        for side, z in ((0, 0), (1, NZ - 1)):
            for n in range(2):
                r = (side * NF + f) * 2 + n
                payload[36 + r // 8, r % 8 : r % 8 + 1, :] = (
                    0.25 * kf[0:1] * coarse[2 + n, f, z : z + 1]
                )


def fixes(payload, side, f):
    even_x = is_even("gx")
    row_id = lax.broadcasted_iota(jnp.int32, (8, 128), 0)
    r = (side * NF + f) * 2
    odd, even = (payload[36 + r // 8, r % 8 + n : r % 8 + n + 1, :] for n in range(2))
    return jnp.where(
        row_id == pick(even_x, 0, 7), odd, jnp.where(row_id == pick(even_x, 7, 0), even, 0.0)
    )


def assemble(new, mids, deltas, mores, columns, kap):
    even_x = is_even("gx")
    add_ghost(new, 0, [mids[f] for f in range(NF)], kap)
    add_ghost(new, NZ - 1, [mids[NF + f] for f in range(NF)], kap)
    for n, first in enumerate((even_x, jnp.logical_not(even_x))):
        here = pick(first, 0, NX - 1)
        inner = pick(first, 1, NX - 2)
        for f in range(NF):
            for h in range(2):
                at = 2 * f + h
                set_row(new, f, h, here, row_of(new, f, h, here) + mores[n, at])
                set_row(new, f, h, inner, row_of(new, f, h, inner) + deltas[n, at])
    add_columns(new, stacked(columns, 0), stacked(columns, 2))


def used_flags(owner):
    row = lax.axis_index("gx")
    col = lax.axis_index("gy")
    size = lax.axis_size("gy")
    left = owner[row, lax.rem(col + size - 1, size)] == 1
    self_used = owner[row, col] == 0
    right = owner[row, lax.rem(col + 1, size)] == -1
    return left, self_used, right


def coarse_kernel(
    c, new_in, payload, sums, mids, deltas, mores, columns, owner, kap, rates,
    out, fine_out, base, new, full, sems,
):
    assemble(new, mids, deltas, mores, columns, kap)
    copies = [
        pltpu.make_async_copy(new.at[:, h], fine_out.at[:, :, h * 128 : (h + 1) * 128], sems.at[h])
        for h in range(2)
    ]
    for copy in copies:
        copy.start()
    for slot, used in enumerate(used_flags(owner)):
        for k in (0, 1, 2, 3, 8, 9, 10, 11):
            tiles = [c[slot, g, k] for g in range(NF)]
            for f in range(NF):
                kf = kap[f]
                near = None
                count = 0.0
                if k not in (0, HIGH):
                    near = c[slot, f, k - 1]
                    count += 1.0
                if k not in (LOW, 11):
                    above = c[slot, f, k + 1]
                    near = above if near is None else near + above
                    count += 1.0
                value = reacted(tiles, f, 1.0, 1.0 - count * kf, rates) + kf * near
                if k in (LOW, HIGH):
                    beyond = c[slot, f, k + 1 if k == LOW else k - 1]
                    value = value - (0.5 * kf) * (tiles[f] + value + kf * (beyond - tiles[f]))
                    if slot != 1:
                        value = jnp.where(used, value, tiles[f])
                        base[slot // 2, f, k - LOW] = value
                    if slot == 1 and k == LOW:
                        value = value - sums[f] + fixes(payload, 0, f)
                    if slot == 1 and k == HIGH:
                        value = value + sums[NF + f] + fixes(payload, 1, f)
                full[slot, f, k] = jnp.where(used, value, tiles[f])
        for f in range(NF):
            for k in range(4, 8):
                value = c[slot, f, k]
                if slot == 1:
                    value = jnp.where(used, payload[f * 4 + k - 4], value)
                else:
                    base[slot // 2, f, k - LOW] = value
                full[slot, f, k] = value
        copy = pltpu.make_async_copy(full.at[slot], out.at[slot], sems.at[2 + slot])
        copy.start()
        copies.append(copy)
    for copy in copies:
        copy.wait()


def finish_kernel(out_in, base, odd, even, y_odd, y_even, shared, out, fixed, sems):
    kap = Shared(shared)
    even_y = is_even("gy")
    copies = []
    for n, slot in enumerate((0, 2)):
        used = kap.flag(2 + n)
        at_odd = even_y if n == 0 else jnp.logical_not(even_y)
        for f in range(NF):
            values = [pick(at_odd, odd[f * 4 + k], even[f * 4 + k]) for k in range(4)]
            low = pick(at_odd, fixes(odd, 0, f) - y_odd[20 + f], fixes(even, 0, f) - y_even[20 + f])
            high = pick(
                at_odd,
                fixes(odd, 1, f) + y_odd[20 + NF + f],
                fixes(even, 1, f) + y_even[20 + NF + f],
            )
            values = [base[n, f, 0] + low] + values + [base[n, f, 5] + high]
            for k in range(6):
                fixed[n, f, k] = jnp.where(used, values[k], base[n, f, k])
        copy = pltpu.make_async_copy(fixed.at[n], out.at[slot, :, LOW : HIGH + 1], sems.at[n])
        copy.start()
        copies.append(copy)
    for copy in copies:
        copy.wait()


def swapped(value, axis, odd):
    size = lax.axis_size(axis)
    pairs = []
    for i in range(odd, size, 2):
        j = (i + 1) % size
        pairs += [(i, j), (j, i)]
    return lax.ppermute(value, axis, pairs)


def on_device(fine_state, coarse_column_state, diffusivity, rates, owner_offset):
    fine_shape = fine_state.shape
    u_in = fine_state.reshape(NF, NZ * NX, NY)
    c = coarse_column_state
    split = (NF, 2, NZ * NX, 128)
    two = (2, 18, 8, 128)
    dma = pltpu.SemaphoreType.DMA

    def tiles(n):
        return (n, 8, 128)

    u, odd, even, own, packs = call(
        prep_kernel,
        [u_in.shape, tiles(20), tiles(20), tiles(18), tiles(4)],
        [pltpu.HBM, pltpu.HBM],
        1 << 20,
        limit=52,
        scratch=[dma((9,))],
    )(c, u_in)
    odd = swapped(odd, "gy", 1)
    even = swapped(even, "gy", 0)
    w, u, packs_w, sums_w, y_odd, y_even, own_mid, shared = call(
        inner1_kernel,
        [split, split] + [tiles(n) for n in (4, 18, 38, 38, 18, Shared.count)],
        [VMEM] * 2 + [SMEM] * 3,
        1 << 27,
        scratch=[pltpu.VMEM((18, 8, NY), F32)],
    )(u, c, diffusivity, rates, owner_offset)
    y_odd, y_even, x_odd, x_even, old, packs1, columns, sums = call(
        edges_kernel,
        [tiles(n) for n in (38, 38, 40, 40, 18, 4, 4, 18)],
        [VMEM] * 11,
        1 << 26,
        aliases={8: 0, 9: 1},
        scratch=[pltpu.VMEM((2, NX, 128), F32)],
    )(u, w, odd, even, own, packs, packs_w, sums_w, y_odd, y_even, shared)
    y_odd = swapped(y_odd, "gy", 1)
    x_odd = swapped(x_odd, "gx", 1)
    y_even = swapped(y_even, "gy", 0)
    x_even = swapped(x_even, "gx", 0)
    u1, new, averages = call(
        inner2_kernel,
        [split, split, tiles(36)],
        [VMEM] * 4,
        1 << 27,
        aliases={0: 0},
        scratch=[pltpu.VMEM((36, 8, NY), F32)],
    )(w, old, columns, shared)
    payload, mids, deltas, mores, columns = call(
        payload_kernel,
        [tiles(41), tiles(18), two, two, tiles(4)],
        [VMEM] * 10,
        1 << 26,
        scratch=[pltpu.VMEM((2, NX, 128), F32), pltpu.VMEM((4, NF, NZ, NY), F32)],
    )(
        u, u1, averages, x_odd, x_even, y_odd, y_even, own_mid, packs1, shared,
    )
    odd = swapped(payload, "gy", 1)
    even = swapped(payload, "gy", 0)
    out, fine_new, base, _ = call(
        coarse_kernel,
        [c.shape, u_in.shape, (2, NF, 6, 8, 128), split],
        [VMEM] * 8 + [SMEM] * 3,
        1 << 26,
        aliases={1: 3},
        scratch=[pltpu.VMEM(c.shape, F32), dma((5,))],
        out_spaces=[pltpu.HBM, pltpu.HBM, VMEM, VMEM],
    )(c, new, payload, sums, mids, deltas, mores, columns, owner_offset, diffusivity, rates)
    (coarse_new,) = call(
        finish_kernel,
        [c.shape],
        [pltpu.HBM] + [VMEM] * 6,
        1 << 20,
        aliases={0: 0},
        scratch=[pltpu.VMEM((2, NF, 6, 8, 128), F32), dma((2,))],
        out_spaces=[pltpu.HBM],
    )(out, base, odd, even, y_odd, y_even, shared)
    return fine_new.reshape(fine_shape), coarse_new


def solution(mesh):
    in_specs = (P(None, None, "gx", "gy"), P(None, None, None, "gx", "gy"), P(), P(), P())
    out_specs = (P(None, None, "gx", "gy"), P(None, None, None, "gx", "gy"))
    return jax.shard_map(
        on_device, mesh=mesh, in_specs=in_specs, out_specs=out_specs, check_vma=False
    )
```

```python
import jax
import jax.numpy as jnp
from jax import lax
from jax.experimental import pallas as pl
from jax.experimental.pallas import tpu as pltpu
from jax.sharding import PartitionSpec as P


F32 = jnp.float32
BF16 = jnp.bfloat16
NF = 9
NZ = 8
NX = 16
NY = 256
LOW = 3
HIGH = 8
VMEM = pltpu.VMEM
SMEM = pltpu.SMEM


def call(kernel, outs, spaces, flops, limit=8, aliases=None, scratch=(), out_spaces=None):
    return pl.pallas_call(
        kernel,
        out_shape=[jax.ShapeDtypeStruct(s, F32) for s in outs],
        in_specs=[pl.BlockSpec(memory_space=s) for s in spaces],
        out_specs=[pl.BlockSpec(memory_space=s) for s in out_spaces or [VMEM] * len(outs)],
        scratch_shapes=list(scratch),
        input_output_aliases=aliases or {},
        compiler_params=pltpu.CompilerParams(vmem_limit_bytes=int(limit * (1 << 20))),
        cost_estimate=pl.CostEstimate(flops=flops, bytes_accessed=1 << 20, transcendentals=0),
    )


def spread_table():
    coarse = lax.broadcasted_iota(jnp.int32, (128, 256), 0)
    fine = lax.broadcasted_iota(jnp.int32, (128, 256), 1)
    return jnp.where(lax.shift_right_logical(fine, 1) == coarse, 1.0, 0.0).astype(BF16)


def gather_table():
    fine = lax.broadcasted_iota(jnp.int32, (256, 128), 0)
    coarse = lax.broadcasted_iota(jnp.int32, (256, 128), 1)
    return jnp.where(lax.shift_right_logical(fine, 1) == coarse, 1.0, 0.0).astype(BF16)


def table_dot(value, table):
    high = value.astype(BF16)
    low = (value - high.astype(F32)).astype(BF16)
    return jnp.dot(high, table, preferred_element_type=F32) + jnp.dot(
        low, table, preferred_element_type=F32
    )


def reacted(tiles, f, scale, diagonal, rates):
    total = tiles[f] * (diagonal + scale * rates[f, f])
    for g in range(NF):
        if g != f:
            total = total + tiles[g] * (scale * rates[f, g])
    return total


def pack_columns(plane_of, side, fields=range(NF), packed=None):
    lane = lax.broadcasted_iota(jnp.int32, (NX, 128), 1)
    if packed is None:
        packed = jnp.zeros((NX, 128), F32)
    for f in fields:
        for z in range(NZ):
            at = z * 16 + f
            shift = at if side == 0 else (at - 127) % 128
            tile = plane_of(f, side, z)
            moved = pltpu.roll(tile, shift, 1) if shift else tile
            packed = jnp.where(lane == at, moved, packed)
    return packed


def split_plane(ref):
    return lambda f, h, z: ref[f, h, z * NX : (z + 1) * NX, :]


def whole_plane(ref):
    return lambda f, h, z: ref[f, z * NX : (z + 1) * NX, h * 128 : (h + 1) * 128]


def put_packs(packs, packed):
    for side in range(2):
        for t in range(2):
            packs[2 * side + t] = packed[side][8 * t : 8 * t + 8]


def kappa_lanes(kap):
    lane = lax.broadcasted_iota(jnp.int32, (NX, 128), 1) & 15
    out = jnp.zeros((NX, 128), F32)
    for f in range(NF):
        out = jnp.where(lane == f, 2.0 * kap[f], out)
    return out


def add_columns(ref, left, right):
    lane = lax.broadcasted_iota(jnp.int32, (NX, 128), 1)
    for z in range(NZ):
        rows = slice(z * NX, (z + 1) * NX)
        for f in range(NF):
            at = z * 16 + f
            moved = pltpu.roll(left, 128 - at, 1) if at else left
            ref[f, 0, rows, :] = ref[f, 0, rows, :] + jnp.where(lane == 0, moved, 0.0)
            shift = 127 - at
            moved = pltpu.roll(right, shift, 1) if shift else right
            ref[f, 1, rows, :] = ref[f, 1, rows, :] + jnp.where(lane == 127, moved, 0.0)


def row_of(ref, f, half, row):
    return ref[f, half, pl.ds(row, NZ, stride=NX), :]


def set_row(ref, f, half, row, value):
    ref[f, half, pl.ds(row, NZ, stride=NX), :] = value


def plane_at(z):
    start = z * NX
    return pl.ds(start if isinstance(z, int) else pl.multiple_of(start, NX), NX)


def substep(src, dst, mixed, k2, copy=None):
    lane = lax.broadcasted_iota(jnp.int32, (NX, 128), 1)

    def tile(f, h, z):
        if copy is None:
            return src[f, h, plane_at(z), :]
        return src[f, plane_at(z), h * 128 : (h + 1) * 128]

    def body(z, others):
        halves = [[tile(g, h, z) for g in range(NF)] for h in range(2)]
        for f in range(NF):
            a, b = halves[0][f], halves[1][f]
            a_up, b_up = pltpu.roll(a, 1, 1), pltpu.roll(b, 1, 1)
            a_down, b_down = pltpu.roll(a, 127, 1), pltpu.roll(b, 127, 1)
            sides = (
                jnp.where(lane == 0, b_up, a_up) + jnp.where(lane == 127, b_down, a_down),
                jnp.where(lane == 0, a_up, b_up) + jnp.where(lane == 127, a_down, b_down),
            )
            for h in range(2):
                v = halves[h][f]
                if copy is not None:
                    copy[f, h, plane_at(z), :] = v
                near = pltpu.roll(v, 1, 0) + pltpu.roll(v, NX - 1, 0) + sides[h]
                for other in others:
                    near = near + tile(f, h, other)
                dst[f, h, plane_at(z), :] = mixed(halves[h], f) + k2(f) * near

    body(0, (1,))

    def step(z, carry):
        body(z, (z - 1, z + 1))
        return carry

    lax.fori_loop(1, NZ - 1, step, 0)
    body(NZ - 1, (NZ - 2,))


def add_ghost(dst, z, tiles, kap):
    wide = table_dot(jnp.concatenate(tiles, axis=0), spread_table())
    for f in range(NF):
        for h in range(2):
            part = (2.0 * kap[f]) * wide[f * 8 : f * 8 + 8, h * 128 : (h + 1) * 128]
            for x in range(2):
                rows = pl.ds(z * NX + x, 8, stride=2)
                dst[f, h, rows, :] = dst[f, h, rows, :] + part


def is_even(axis):
    return (lax.axis_index(axis) & 1) == 0


def pick(flag, one, other):
    return jnp.where(flag, one, other)


def prep_kernel(c, u_in, u, odd, even, own, packs, sems):
    even_y = is_even("gy")
    fine = [
        pltpu.make_async_copy(u_in.at[3 * n : 3 * n + 3], u.at[3 * n : 3 * n + 3], sems.at[n])
        for n in range(3)
    ]
    copies = []
    for n, (slot, dst) in enumerate(((pick(even_y, 0, 2), odd), (pick(even_y, 2, 0), even), (1, own))):
        for side, k in ((0, LOW), (1, HIGH)):
            copies.append(
                pltpu.make_async_copy(
                    c.at[slot, :, k], dst.at[pl.ds(side * NF, NF)], sems.at[3 + 2 * n + side]
                )
            )
    for copy in fine + copies:
        copy.start()
    packed = [None, None]
    for n, copy in enumerate(fine):
        copy.wait()
        packed = [
            pack_columns(whole_plane(u), side, range(3 * n, 3 * n + 3), packed[side])
            for side in range(2)
        ]
    put_packs(packs, packed)
    for t in range(2):
        left, right = (packed[side][8 * t : 8 * t + 8] for side in range(2))
        odd[18 + t] = pick(even_y, left, right)
        even[18 + t] = pick(even_y, right, left)
    for copy in copies:
        copy.wait()


def pair_rows(ref, f, half, z):
    return (
        ref[f, half, pl.ds(z * NX, 8, stride=2), :]
        + ref[f, half, pl.ds(z * NX + 1, 8, stride=2), :]
    )


def tall(tile):
    return jnp.concatenate([tile, tile], axis=0)


class Shared:
    count = 95

    def __init__(self, ref):
        self.ref = ref

    def __getitem__(self, f):
        return self.ref[81 + f]

    def lanes(self):
        return self.ref[90]

    def flag(self, n):
        return self.ref[91 + n] > 0.5

    def mixed(self, tiles, f):
        total = tiles[0] * self.ref[f * NF]
        for g in range(1, NF):
            total = total + tiles[g] * self.ref[f * NF + g]
        return total

    def mixed_tall(self, tiles, f):
        total = tiles[0] * tall(self.ref[f * NF])
        for g in range(1, NF):
            total = total + tiles[g] * tall(self.ref[f * NF + g])
        return total


def fill_shared(shared, owner, kap, rates):
    for f in range(NF):
        for g in range(NF):
            value = 0.5 * rates[f, g]
            if f == g:
                value = value + (1.0 - 12.0 * kap[f])
            shared[f * NF + g] = jnp.full((8, 128), value, F32)
        shared[81 + f] = jnp.full((8, 128), kap[f], F32)
    shared[90] = kappa_lanes(kap)[0:8]
    mine = owner[lax.axis_index("gx"), lax.axis_index("gy")]
    left, _, right = used_flags(owner)
    flags = (mine == 0, mine == pick(is_even("gy"), -1, 1), left, right)
    for n, flag in enumerate(flags):
        shared[91 + n] = jnp.full((8, 128), jnp.where(flag, 1.0, 0.0), F32)


def inner1_kernel(
    u_in, c, kap, rates, owner, w, u, packs, sums, odd, even, own, shared, pairs
):
    fill_shared(shared, owner, kap, rates)
    substep(
        u_in,
        w,
        lambda tiles, f: reacted(tiles, f, 0.5, 1.0 - 12.0 * kap[f], rates),
        lambda f: 2.0 * kap[f],
        u,
    )
    for f in range(NF):
        k2 = 2.0 * kap[f]
        for h in range(2):
            set_row(w, f, h, 0, row_of(w, f, h, 0) - k2 * row_of(u, f, h, NX - 1))
            set_row(w, f, h, NX - 1, row_of(w, f, h, NX - 1) - k2 * row_of(u, f, h, 0))
    put_packs(packs, [pack_columns(split_plane(w), side) for side in range(2)])
    for side, z in ((0, 0), (1, NZ - 1)):
        for f in range(NF):
            for h in range(2):
                pairs[side * NF + f, :, h * 128 : (h + 1) * 128] = pair_rows(u, f, h, z) + pair_rows(
                    w, f, h, z
                )
    coarse = table_dot(pairs[...].reshape(18 * 8, NY), gather_table())
    for t in range(18):
        sums[t] = 0.25 * coarse[t * 8 : t * 8 + 8]
    even_y = is_even("gy")
    for slot, dst in ((pick(even_y, 0, 2), odd), (1, own), (pick(even_y, 2, 0), even)):
        for side, k in ((0, LOW), (1, HIGH)):
            tiles = [c[slot, g, k] for g in range(NF)]
            for f in range(NF):
                kf = kap[f]
                near = c[slot, f, k - 1] + c[slot, f, k + 1]
                dst[side * NF + f] = (
                    reacted(tiles, f, 0.5, 1.0 - kf, rates) + (0.5 * kf) * near
                )


def chosen(shared, odd, even, own, rims):
    at_own = shared.flag(0)
    at_odd = shared.flag(1)
    for t in range(18):
        rims[t] = jnp.where(at_own, own[t], jnp.where(at_odd, odd[t], even[t]))


def stacked(ref, at):
    return jnp.concatenate([ref[at], ref[at + 1]], axis=0)


def refined(tiles):
    return table_dot(jnp.concatenate(tiles, axis=0), spread_table())


def edges_kernel(
    u, w, odd_in, even_in, own, packs, packs_w, sums_w, y_odd_in, y_even_in, shared,
    y_odd, y_even, x_odd, x_even, rims, packs1, columns, sums, ghost,
):
    even_y = is_even("gy")
    even_x = is_even("gx")
    kap = Shared(shared)
    chosen(kap, odd_in, even_in, own, rims)
    k_lanes = tall(kap.lanes())
    odd, even = stacked(odd_in, 18), stacked(even_in, 18)
    from_left = pick(even_y, odd, even)
    from_right = pick(even_y, even, odd)
    left = k_lanes * (from_left - stacked(packs, 2))
    right = k_lanes * (from_right - stacked(packs, 0))
    put_packs(columns, [left, right])
    lane = lax.broadcasted_iota(jnp.int32, (8, 128), 1)
    for side in range(2):
        packed = jnp.zeros((8, 128), F32)
        for f in range(NF):
            for at, tile in ((f, rims[f]), (112 + f, rims[NF + f])):
                shift = at if side == 0 else (at - 127) % 128
                moved = pltpu.roll(tile, shift, 1) if shift else tile
                packed = jnp.where(lane == at, moved, packed)
        packed = packed * k_lanes[0:8]
        ghost[side, pl.ds(0, 8, stride=2), :] = packed
        ghost[side, pl.ds(1, 8, stride=2), :] = packed
    new_left = stacked(packs_w, 0) + left + ghost[0]
    new_right = stacked(packs_w, 2) + right + ghost[1]
    put_packs(packs1, [new_left, new_right])
    for t in range(2):
        a, b = new_left[8 * t : 8 * t + 8], new_right[8 * t : 8 * t + 8]
        y_odd[18 + t] = pick(even_y, a, b)
        y_even[18 + t] = pick(even_y, b, a)
    totals = []
    for side, value in enumerate((left, right)):
        ghost[side] = value
        totals.append(
            0.25 * (ghost[side, pl.ds(0, 8, stride=2), :] + ghost[side, pl.ds(1, 8, stride=2), :])
        )
    for side in range(2):
        for f in range(NF):
            kf = kap[f]
            at = 112 * side + f
            a = pltpu.roll(totals[0], 128 - at, 1) if at else totals[0]
            b = pltpu.roll(totals[1], 127 - at, 1)
            t = side * NF + f
            flux = sums_w[t] + jnp.where(lane == 0, a, jnp.where(lane == 127, b, 0.0))
            flux = flux + (2.0 * kf - 1.0) * rims[t]
            value = (-kf if side == 0 else kf) * flux
            sums[t] = value
            y_odd[20 + t] = value
            y_even[20 + t] = value
    wide_low = refined([rims[f] for f in range(NF)])
    wide_high = refined([rims[NF + f] for f in range(NF)])
    layer = lax.broadcasted_iota(jnp.int32, (NZ, 128), 0)
    for f in range(NF):
        k2 = 2.0 * kap[f]
        for h in range(2):
            lanes = slice(h * 128, (h + 1) * 128)
            first = row_of(u, f, h, 0)
            last = row_of(u, f, h, NX - 1)
            values = []
            for row, at in ((0, f * 8), (NX - 1, f * 8 + 7)):
                more = jnp.where(
                    layer == 0,
                    wide_low[at : at + 1, lanes],
                    jnp.where(layer == NZ - 1, wide_high[at : at + 1, lanes], 0.0),
                )
                values.append(row_of(w, f, h, row) + k2 * more)
            x_odd[2 * f + h] = pick(even_x, first, last)
            x_odd[18 + 2 * f + h] = pick(even_x, values[0], values[1])
            x_even[2 * f + h] = pick(even_x, last, first)
            x_even[18 + 2 * f + h] = pick(even_x, values[1], values[0])
    row_id = lax.broadcasted_iota(jnp.int32, (8, 128), 0)
    top = jnp.where(row_id == 0, left[0:1], right[0:1])
    bottom = jnp.where(row_id == 0, left[NX - 1 : NX], right[NX - 1 : NX])
    x_odd[36] = pick(even_x, top, bottom)
    x_even[36] = pick(even_x, bottom, top)


def inner2_kernel(w, rims, columns, shared, u1, new, averages, sums):
    kap = Shared(shared)
    add_ghost(u1, 0, [rims[f] for f in range(NF)], kap)
    add_ghost(u1, NZ - 1, [rims[NF + f] for f in range(NF)], kap)
    add_columns(u1, stacked(columns, 0), stacked(columns, 2))
    substep(u1, new, kap.mixed_tall, lambda f: tall(2.0 * kap[f]))
    for f in range(NF):
        for h in range(2):
            lanes = slice(h * 128, (h + 1) * 128)
            for c in range(4):
                sums[f * 4 + c, :, lanes] = pair_rows(new, f, h, 2 * c) + pair_rows(
                    new, f, h, 2 * c + 1
                )
    table = gather_table()
    for f in range(NF):
        coarse = table_dot(sums[f * 4 : f * 4 + 4].reshape(32, NY), table)
        for c in range(4):
            averages[f * 4 + c] = coarse[c * 8 : c * 8 + 8] * 0.125


def row_terms(u, u1, message, kap, first, deltas, mores):
    here = pick(first, 0, NX - 1)
    opposite = pick(first, NX - 1, 0)
    layer = lax.broadcasted_iota(jnp.int32, (NZ, 128), 0)
    lane = lax.broadcasted_iota(jnp.int32, (NZ, 128), 1)
    delta = [[2.0 * kap[g] * message[2 * g + h] for g in range(NF)] for h in range(2)]
    for f in range(NF):
        k = kap[f]
        k2 = 2.0 * k
        a, b = delta[0][f], delta[1][f]
        a_up, b_up = pltpu.roll(a, 1, 1), pltpu.roll(b, 1, 1)
        a_down, b_down = pltpu.roll(a, 127, 1), pltpu.roll(b, 127, 1)
        sides = (
            jnp.where(lane == 0, b_up, a_up) + jnp.where(lane == 127, b_down, a_down),
            jnp.where(lane == 0, a_up, b_up) + jnp.where(lane == 127, a_down, b_down),
        )
        for h in range(2):
            d = delta[h][f]
            near = sides[h] + jnp.where(layer == 0, 0.0, pltpu.roll(d, 1, 0))
            near = near + jnp.where(layer == NZ - 1, 0.0, pltpu.roll(d, NZ - 1, 0))
            halo = message[18 + 2 * f + h] + k2 * row_of(u, f, h, here)
            near = near + (halo - row_of(u1, f, h, opposite))
            more = kap.mixed(delta[h], f) + k2 * near
            deltas[2 * f + h] = k2 * d
            mores[2 * f + h] = more
    return delta


def payload_kernel(
    u, u1, averages, x_odd, x_even, y_odd, y_even, own_mid, packs1, shared,
    payload, mids, deltas, mores, columns, pairs, rows,
):
    even_y = is_even("gy")
    even_x = is_even("gx")
    kap = Shared(shared)
    chosen(kap, y_odd, y_even, own_mid, mids)
    row_odd = pick(even_x, 0, 7)
    row_even = pick(even_x, 7, 0)
    for n, (message, first) in enumerate(((x_odd, even_x), (x_even, jnp.logical_not(even_x)))):
        delta = row_terms(u, u1, message, kap, first, deltas.at[n], mores.at[n])
        for f in range(NF):
            for h in range(2):
                lanes = slice(h * 128, (h + 1) * 128)
                rows[n, f, :, lanes] = mores[n, 2 * f + h] + deltas[n, 2 * f + h]
                rows[2 + n, f, :, lanes] = delta[h][f]
    table = gather_table()
    coarse = table_dot(rows[...].reshape(4 * NF * NZ, NY), table).reshape(4, NF, NZ, 128)
    k_lanes = tall(kap.lanes())
    x_id = lax.broadcasted_iota(jnp.int32, (NX, 128), 0)

    low = pick(even_x, x_odd[36], x_even[36])
    high = pick(even_x, x_even[36], x_odd[36])

    def corner(n):
        at_high = jnp.where(x_id == NX - 1, high[n : n + 1], 0.0)
        return 2.0 * jnp.where(x_id == 0, low[n : n + 1], at_high)

    odd, even = stacked(y_odd, 18), stacked(y_even, 18)
    left = pick(even_y, odd, even) - stacked(packs1, 2) + corner(0)
    right = pick(even_y, even, odd) - stacked(packs1, 0) + corner(1)
    left = k_lanes * left
    right = k_lanes * right
    put_packs(columns, [left, right])
    side_sums = []
    for n, value in enumerate((left, right)):
        pairs[n] = value
        total = pairs[n, pl.ds(0, 8, stride=2), :] + pairs[n, pl.ds(1, 8, stride=2), :]
        side_sums.append(0.125 * (total + pltpu.roll(total, 112, 1)))
    row_id = lax.broadcasted_iota(jnp.int32, (8, 128), 0)
    lane = lax.broadcasted_iota(jnp.int32, (8, 128), 1)
    at_odd = row_id == row_odd
    at_even = row_id == row_even
    for f in range(NF):
        kf = kap[f]
        halves = [0.125 * (coarse[n, f] + pltpu.roll(coarse[n, f], NZ - 1, 0)) for n in range(2)]
        for c in range(4):
            value = averages[f * 4 + c]
            if c == 0:
                value = value + kf * mids[f]
            if c == 3:
                value = value + kf * mids[NF + f]
            z = 2 * c
            value = value + jnp.where(
                at_odd, halves[0][z : z + 1], jnp.where(at_even, halves[1][z : z + 1], 0.0)
            )
            at = z * 16 + f
            a = pltpu.roll(side_sums[0], 128 - at, 1) if at else side_sums[0]
            b = pltpu.roll(side_sums[1], 127 - at, 1) if at != 127 else side_sums[1]
            value = value + jnp.where(lane == 0, a, jnp.where(lane == 127, b, 0.0))
            payload[f * 4 + c] = value
        for side, z in ((0, 0), (1, NZ - 1)):
            for n in range(2):
                r = (side * NF + f) * 2 + n
                payload[36 + r // 8, r % 8 : r % 8 + 1, :] = (
                    0.25 * kf[0:1] * coarse[2 + n, f, z : z + 1]
                )


def fixes(payload, side, f):
    even_x = is_even("gx")
    row_id = lax.broadcasted_iota(jnp.int32, (8, 128), 0)
    r = (side * NF + f) * 2
    odd, even = (payload[36 + r // 8, r % 8 + n : r % 8 + n + 1, :] for n in range(2))
    return jnp.where(
        row_id == pick(even_x, 0, 7), odd, jnp.where(row_id == pick(even_x, 7, 0), even, 0.0)
    )


def assemble(new, mids, deltas, mores, columns, kap):
    even_x = is_even("gx")
    add_ghost(new, 0, [mids[f] for f in range(NF)], kap)
    add_ghost(new, NZ - 1, [mids[NF + f] for f in range(NF)], kap)
    for n, first in enumerate((even_x, jnp.logical_not(even_x))):
        here = pick(first, 0, NX - 1)
        inner = pick(first, 1, NX - 2)
        for f in range(NF):
            for h in range(2):
                at = 2 * f + h
                set_row(new, f, h, here, row_of(new, f, h, here) + mores[n, at])
                set_row(new, f, h, inner, row_of(new, f, h, inner) + deltas[n, at])
    add_columns(new, stacked(columns, 0), stacked(columns, 2))


def used_flags(owner):
    row = lax.axis_index("gx")
    col = lax.axis_index("gy")
    size = lax.axis_size("gy")
    left = owner[row, lax.rem(col + size - 1, size)] == 1
    self_used = owner[row, col] == 0
    right = owner[row, lax.rem(col + 1, size)] == -1
    return left, self_used, right


def coarse_kernel(
    c, new_in, payload, sums, mids, deltas, mores, columns, owner, kap, rates,
    out, fine_out, base, new, full, sems,
):
    assemble(new, mids, deltas, mores, columns, kap)
    copies = [
        pltpu.make_async_copy(new.at[:, h], fine_out.at[:, :, h * 128 : (h + 1) * 128], sems.at[h])
        for h in range(2)
    ]
    for copy in copies:
        copy.start()
    for slot, used in enumerate(used_flags(owner)):
        for k in (0, 1, 2, 3, 8, 9, 10, 11):
            tiles = [c[slot, g, k] for g in range(NF)]
            for f in range(NF):
                kf = kap[f]
                near = None
                count = 0.0
                if k not in (0, HIGH):
                    near = c[slot, f, k - 1]
                    count += 1.0
                if k not in (LOW, 11):
                    above = c[slot, f, k + 1]
                    near = above if near is None else near + above
                    count += 1.0
                value = reacted(tiles, f, 1.0, 1.0 - count * kf, rates) + kf * near
                if k in (LOW, HIGH):
                    beyond = c[slot, f, k + 1 if k == LOW else k - 1]
                    value = value - (0.5 * kf) * (tiles[f] + value + kf * (beyond - tiles[f]))
                    if slot != 1:
                        value = jnp.where(used, value, tiles[f])
                        base[slot // 2, f, k - LOW] = value
                    if slot == 1 and k == LOW:
                        value = value - sums[f] + fixes(payload, 0, f)
                    if slot == 1 and k == HIGH:
                        value = value + sums[NF + f] + fixes(payload, 1, f)
                full[slot, f, k] = jnp.where(used, value, tiles[f])
        for f in range(NF):
            for k in range(4, 8):
                value = c[slot, f, k]
                if slot == 1:
                    value = jnp.where(used, payload[f * 4 + k - 4], value)
                else:
                    base[slot // 2, f, k - LOW] = value
                full[slot, f, k] = value
        copy = pltpu.make_async_copy(full.at[slot], out.at[slot], sems.at[2 + slot])
        copy.start()
        copies.append(copy)
    for copy in copies:
        copy.wait()


def finish_kernel(out_in, base, odd, even, y_odd, y_even, shared, out, fixed, sems):
    kap = Shared(shared)
    even_y = is_even("gy")
    copies = []
    for n, slot in enumerate((0, 2)):
        used = kap.flag(2 + n)
        at_odd = even_y if n == 0 else jnp.logical_not(even_y)
        for f in range(NF):
            values = [pick(at_odd, odd[f * 4 + k], even[f * 4 + k]) for k in range(4)]
            low = pick(at_odd, fixes(odd, 0, f) - y_odd[20 + f], fixes(even, 0, f) - y_even[20 + f])
            high = pick(
                at_odd,
                fixes(odd, 1, f) + y_odd[20 + NF + f],
                fixes(even, 1, f) + y_even[20 + NF + f],
            )
            values = [base[n, f, 0] + low] + values + [base[n, f, 5] + high]
            for k in range(6):
                fixed[n, f, k] = jnp.where(used, values[k], base[n, f, k])
        copy = pltpu.make_async_copy(fixed.at[n], out.at[slot, :, LOW : HIGH + 1], sems.at[n])
        copy.start()
        copies.append(copy)
    for copy in copies:
        copy.wait()


def swapped(value, axis, odd):
    size = lax.axis_size(axis)
    pairs = []
    for i in range(odd, size, 2):
        j = (i + 1) % size
        pairs += [(i, j), (j, i)]
    return lax.ppermute(value, axis, pairs)


def on_device(fine_state, coarse_column_state, diffusivity, rates, owner_offset):
    fine_shape = fine_state.shape
    u_in = fine_state.reshape(NF, NZ * NX, NY)
    c = coarse_column_state
    split = (NF, 2, NZ * NX, 128)
    two = (2, 18, 8, 128)
    dma = pltpu.SemaphoreType.DMA

    def tiles(n):
        return (n, 8, 128)

    u, odd, even, own, packs = call(
        prep_kernel,
        [u_in.shape, tiles(20), tiles(20), tiles(18), tiles(4)],
        [pltpu.HBM, pltpu.HBM],
        1 << 20,
        limit=52,
        scratch=[dma((9,))],
    )(c, u_in)
    odd = swapped(odd, "gy", 1)
    even = swapped(even, "gy", 0)
    w, u, packs_w, sums_w, y_odd, y_even, own_mid, shared = call(
        inner1_kernel,
        [split, split] + [tiles(n) for n in (4, 18, 38, 38, 18, Shared.count)],
        [VMEM] * 2 + [SMEM] * 3,
        1 << 27,
        scratch=[pltpu.VMEM((18, 8, NY), F32)],
    )(u, c, diffusivity, rates, owner_offset)
    y_odd, y_even, x_odd, x_even, old, packs1, columns, sums = call(
        edges_kernel,
        [tiles(n) for n in (38, 38, 37, 37, 18, 4, 4, 18)],
        [VMEM] * 11,
        1 << 26,
        aliases={8: 0, 9: 1},
        scratch=[pltpu.VMEM((2, NX, 128), F32)],
    )(u, w, odd, even, own, packs, packs_w, sums_w, y_odd, y_even, shared)
    y_odd = swapped(y_odd, "gy", 1)
    x_odd = swapped(x_odd, "gx", 1)
    y_even = swapped(y_even, "gy", 0)
    x_even = swapped(x_even, "gx", 0)
    u1, new, averages = call(
        inner2_kernel,
        [split, split, tiles(36)],
        [VMEM] * 4,
        1 << 27,
        aliases={0: 0},
        scratch=[pltpu.VMEM((36, 8, NY), F32)],
    )(w, old, columns, shared)
    payload, mids, deltas, mores, columns = call(
        payload_kernel,
        [tiles(41), tiles(18), two, two, tiles(4)],
        [VMEM] * 10,
        1 << 26,
        scratch=[pltpu.VMEM((2, NX, 128), F32), pltpu.VMEM((4, NF, NZ, NY), F32)],
    )(
        u, u1, averages, x_odd, x_even, y_odd, y_even, own_mid, packs1, shared,
    )
    odd = swapped(payload, "gy", 1)
    even = swapped(payload, "gy", 0)
    out, fine_new, base, _ = call(
        coarse_kernel,
        [c.shape, u_in.shape, (2, NF, 6, 8, 128), split],
        [VMEM] * 8 + [SMEM] * 3,
        1 << 26,
        aliases={1: 3},
        scratch=[pltpu.VMEM(c.shape, F32), dma((5,))],
        out_spaces=[pltpu.HBM, pltpu.HBM, VMEM, VMEM],
    )(c, new, payload, sums, mids, deltas, mores, columns, owner_offset, diffusivity, rates)
    (coarse_new,) = call(
        finish_kernel,
        [c.shape],
        [pltpu.HBM] + [VMEM] * 6,
        1 << 20,
        aliases={0: 0},
        scratch=[pltpu.VMEM((2, NF, 6, 8, 128), F32), dma((2,))],
        out_spaces=[pltpu.HBM],
    )(out, base, odd, even, y_odd, y_even, shared)
    return fine_new.reshape(fine_shape), coarse_new


def solution(mesh):
    in_specs = (P(None, None, "gx", "gy"), P(None, None, None, "gx", "gy"), P(), P(), P())
    out_specs = (P(None, None, "gx", "gy"), P(None, None, None, "gx", "gy"))
    return jax.shard_map(
        on_device, mesh=mesh, in_specs=in_specs, out_specs=out_specs, check_vma=False
    )
```
